32 devices in a mesh: groups: 1, dp: 32 (over z, y, x, core).
Axes of the slice: x: 2, y: 2, z: 4, core: 2. Of those that a mesh axis runs over, the one named last changes fastest.
Arguments:
- activations: bfloat16 [128, 8192], P(('groups', 'dp')), may hold values from -6 to 6
- cotangent: bfloat16 [128, 8192], P(('groups', 'dp')), may hold values from -6 to 6
- w_gate: bfloat16 [28672, 8192], P('dp'), may hold values from -0.0625 to 0.0625
- w_up: bfloat16 [28672, 8192], P('dp'), may hold values from -0.0625 to 0.0625
- w_down: bfloat16 [28672, 8192], P('dp'), may hold values from -0.03125 to 0.03125
- proj_model: bfloat16 [8192, 192], P('dp'), may hold values from -0.0625 to 0.0625
- proj_hidden: bfloat16 [28672, 192], P('dp'), may hold values from -0.03125 to 0.03125
- seq_ids: int32 [128], P('groups'), may hold values from 0 to 15, never falling along the last dimension, each value on 1 to 16 neighbouring positions
- targets: bfloat16 [256, 3, 64, 64], P(('groups', 'dp')), may hold values from -24 to 24
- target_domain: int32 [256], P(('groups', 'dp')), may hold values from 0 to 31, never falling along the last dimension, each value on 1 to 16 neighbouring positions
Outputs:
- sketches: float32 [16, 3, 64, 64], P('groups')
- scores: float32 [16, 32], P('groups')
The draws below stay inside these ranges and needn't reach their ends.
Inputs may be any that keep to these rules, and one draw needn't show every extreme that they name: `seq_ids`: never falling along the tokens; each of the 16 sequences has 1 to 16 tokens, one exactly 16. `target_domain`: never falling along the target examples; each of the 32 domains has 1 to 16 examples, one exactly 16.
All inputs are finite; a program needn't handle non-finite values.
Results may differ from the reference program's by a relative error of at most 0.0032.
Values may be sent and summed in bfloat16 or wider, within the bound.
A program may use at most 128 MiB of HBM per device.

```python
import math
import jax
import jax.numpy as jnp
import numpy as np
from jax import lax

D = 8192
FF = 28672
RANK = 64
DOMAINS = 32
SEQS = 16
TOKENS = 128
TARGETS = 256
SEQ_MOST = 16
DOM_MOST = 16


def level_of(own_key, extent, cuts, low, top_value):
    loudness, own = 1.0, jax.random.fold_in(own_key, 6)
    for dim, blocks in cuts:
        steps = jnp.exp(jax.random.uniform(jax.random.fold_in(own, dim), (blocks,), jnp.float32, low / len(cuts), top_value / len(cuts)))
        loudness = loudness * jnp.repeat(steps, extent[dim] // blocks).reshape([-1 if axis == dim else 1 for axis in range(len(extent))])
    return loudness


def length_profile(amount, total, reach, skew):
    portions = [(1 << 20) // math.isqrt(rank ** skew) + 1 for rank in range(2, amount + 1)]
    rest, counts = total - reach - (amount - 1), [1] * (amount - 1)
    while rest > 0:
        candidates = [i for i in range(amount - 1) if counts[i] < reach]
        mass, budget = sum([portions[i] for i in candidates]), rest
        for i in candidates:
            extra = min(reach - counts[i], max(1, budget * portions[i] // mass), rest)
            counts[i] = counts[i] + extra
            rest = rest - extra
    return np.array([reach] + counts)


def ragged_sizes(rng, amount, total, limit, slope):
    if amount == 2:
        one = jax.random.randint(rng, (), max(1, total - limit), min(limit, total - 1) + 1)
        return jnp.stack([one, total - one])
    tallies = jnp.asarray(length_profile(amount, total, limit, slope), jnp.int32)
    couples = (amount - 1) // 2
    source_of, taker = tallies[1:1 + 2 * couples:2], tallies[2:2 + 2 * couples:2]
    room = jnp.minimum(source_of - 1, limit - taker)
    moved = jax.random.randint(jax.random.fold_in(rng, 1), (couples,), 0, 1 << 20) % (room + 1)
    tallies = tallies.at[1:1 + 2 * couples:2].set(source_of - moved).at[2:2 + 2 * couples:2].set(taker + moved)
    return tallies[jax.random.permutation(jax.random.fold_in(rng, 2), amount)]


def bell_draw(key, extent, spread, bound, shards=(), dtype=jnp.bfloat16):
    values = spread * jax.random.normal(key, extent, jnp.float32)
    if shards:
        values = values * level_of(key, extent, shards, -0.22, 0.18)
    return jnp.clip(values, -bound, bound).astype(dtype)


def setup_inputs(seed: int = 0, part: int = 0) -> dict:
    streams_of = jax.random.split(jax.random.key(seed), 11)
    part_splits = jax.random.split(jax.random.fold_in(streams_of[10], part), 11)
    activations = bell_draw(part_splits[0], (TOKENS, D), 1.0, 6.0, ((0, 32),))
    cotangent = bell_draw(part_splits[1], (TOKENS, D), 1.0, 6.0, ((0, 32),))
    w_gate = bell_draw(streams_of[2], (FF, D), D ** -0.5, 0.0625, ((0, 32),))
    w_up = bell_draw(streams_of[3], (FF, D), D ** -0.5, 0.0625, ((0, 32),))
    w_down = bell_draw(streams_of[4], (FF, D), FF ** -0.5, 0.03125, ((0, 32),))
    proj_model = bell_draw(streams_of[5], (D, 3 * RANK), D ** -0.5, 0.0625, ((0, 32),))
    proj_hidden = bell_draw(streams_of[6], (FF, 3 * RANK), FF ** -0.5, 0.03125, ((0, 32),))
    seq_ids = jnp.searchsorted(jnp.cumsum(ragged_sizes(part_splits[7], SEQS, TOKENS, SEQ_MOST, 2)), jnp.arange(TOKENS), side="right").astype(jnp.int32)
    targets = bell_draw(part_splits[8], (TARGETS, 3, RANK, RANK), 4.0, 24.0, ((0, 32),))
    target_domain = jnp.searchsorted(jnp.cumsum(ragged_sizes(part_splits[9], DOMAINS, TARGETS, DOM_MOST, 2)), jnp.arange(TARGETS), side="right").astype(jnp.int32)
    return dict(activations=activations, cotangent=cotangent, w_gate=w_gate, w_up=w_up, w_down=w_down, proj_model=proj_model, proj_hidden=proj_hidden, seq_ids=seq_ids, targets=targets, target_domain=target_domain)


def sequence_sketch(vectors, onehot):
    blocks = vectors.reshape(vectors.shape[0], 6, RANK)
    left_side = jnp.stack((blocks[:, 4], blocks[:, 5], blocks[:, 3]), 1)
    right_side = jnp.stack((blocks[:, 0], blocks[:, 1], blocks[:, 2]), 1)
    return jnp.einsum('ns,nka,nkb->skab', onehot, left_side, right_side, precision=lax.Precision.HIGHEST)

def reference(activations, cotangent, w_gate, w_up, w_down, proj_model, proj_hidden, seq_ids, targets, target_domain):
    pieces = 8
    width_block = FF // pieces
    in_model = jnp.dot(activations, proj_model[:, :2 * RANK], preferred_element_type=jnp.float32)
    out_down = jnp.dot(cotangent, proj_model[:, 2 * RANK:], preferred_element_type=jnp.float32)

    def hidden_block(inputs_block):
        gate_rows, up_rows, down_rows, proj_rows = inputs_block
        gate_value = jnp.dot(activations, gate_rows.T, preferred_element_type=jnp.float32)
        up_value = jnp.dot(activations, up_rows.T, preferred_element_type=jnp.float32)
        sigmoid_gate = jax.nn.sigmoid(gate_value)
        silu_gate = gate_value * sigmoid_gate
        hidden = (silu_gate * up_value).astype(jnp.bfloat16)
        grad_hidden = jnp.dot(cotangent, down_rows.T, preferred_element_type=jnp.float32)
        grad_gate = (grad_hidden * up_value * sigmoid_gate * (1.0 + gate_value * (1.0 - sigmoid_gate))).astype(jnp.bfloat16)
        grad_up = (grad_hidden * silu_gate).astype(jnp.bfloat16)
        in_down = jnp.dot(hidden, proj_rows[:, :RANK], preferred_element_type=jnp.float32)
        out_gate = jnp.dot(grad_gate, proj_rows[:, RANK:2 * RANK], preferred_element_type=jnp.float32)
        out_up = jnp.dot(grad_up, proj_rows[:, 2 * RANK:], preferred_element_type=jnp.float32)
        return jnp.concatenate([in_down, out_gate, out_up], 1)
    stacked = (w_gate.reshape(pieces, width_block, D), w_up.reshape(pieces, width_block, D), w_down.reshape(pieces, width_block, D), proj_hidden.reshape(pieces, width_block, 3 * RANK))
    hidden_terms = lax.optimization_barrier(jnp.sum(lax.map(hidden_block, stacked), axis=0))
    vectors = jnp.concatenate([in_model, out_down, hidden_terms], 1)
    onehot = (seq_ids[:, None] == jnp.arange(SEQS)[None, :]).astype(jnp.float32)
    sketches = sequence_sketch(vectors, onehot)
    flat_sketch = sketches.reshape(SEQS, 3 * RANK * RANK)
    domain_onehot = (target_domain[None, :] == jnp.arange(DOMAINS)[:, None]).astype(jnp.bfloat16)
    domain_sum = jnp.dot(domain_onehot, targets.reshape(TARGETS, 3 * RANK * RANK), preferred_element_type=jnp.float32)
    domain_count = lax.optimization_barrier(jnp.sum(domain_onehot.astype(jnp.float32), 1))
    domain_mean = domain_sum / domain_count[:, None]
    inverse_norm = lax.rsqrt(lax.optimization_barrier(jnp.sum(flat_sketch * flat_sketch, 1)) + 1e-06)
    scores = jnp.dot(flat_sketch, domain_mean.T, precision=lax.Precision.HIGHEST) * inverse_norm[:, None]
    return (sketches, scores)
```

```python
import functools

import jax
import jax.numpy as jnp
from jax import lax
from jax.experimental import pallas as pl
from jax.experimental.pallas import tpu as pltpu
from jax.sharding import PartitionSpec as P

DOMAINS = 32
SEQS = 16
MESH = pl.DeviceIdType.MESH
ROUTES = 2
CHUNKS = 8


def routes_of(n):
    core = (2, 1)
    if n == 32:
        z, y, x = (4, 8), (2, 4), (2, 2)
        return ((z, y, x, core), (z, x, y, core))
    if n == 128:
        y, x = (8, 16), (8, 2)
        return ((y, x, core), (x, y, core))
    rest = (n // 2, 2)
    return ((rest, core), (rest, core))


def moved(index, size, stride, by):
    coord = lax.rem(lax.div(index, stride), size)
    return index + (lax.rem(coord + by, size) - coord) * stride


def kernel(
    n,
    act_ref, cot_ref, wg_ref, wu_ref, wd_ref, pm_ref, ph_ref, seq_ref, tgt_ref, dom_ref,
    sk_ref, score_ref,
    wbuf, xg, xs, gacc, uacc, dacc, part, rsbuf, red, vg, lm, prod, msg, msgbuf,
    w_sem, own_sem, ag_send, ag_recv, rs_send, rs_recv, bc_send, bc_recv, sc_send, sc_recv,
):
    me = lax.axis_index("dp")
    half = n // 2
    routes = routes_of(n)
    tokens, width = xs.shape[2], xs.shape[3]
    per_route = CHUNKS // ROUTES
    rank = pm_ref.shape[1] // 3
    hidden_units = wg_ref.shape[0]
    own_rows = act_ref.shape[1]

    def weight_copy(m, c):
        source = (wg_ref, wu_ref, wd_ref)[m]
        return pltpu.make_async_copy(
            source.at[:, pl.ds(c * width, width)], wbuf.at[m, c], w_sem.at[m, c]
        )

    own_copies = []
    for a, source in enumerate((act_ref, cot_ref)):
        for r in range(ROUTES):
            copy = pltpu.make_async_copy(source.at[r], xg.at[a, r, me], own_sem.at[a, r])
            copy.start()
            own_copies.append(copy)

    barrier = pltpu.get_barrier_semaphore()

    def greet(d, carry):
        pl.semaphore_signal(
            barrier, inc=1, device_id={"dp": lax.rem(me + d, n)}, device_id_type=MESH
        )
        return carry

    lax.fori_loop(1, n, greet, 0)
    for c in range(CHUNKS):
        weight_copy(0, c).start()
        weight_copy(1, c).start()
    for c in range(CHUNKS):
        weight_copy(2, c).start()
    for copy in own_copies:
        copy.wait()
    pl.semaphore_wait(barrier, n - 1)

    def held_before(r, stage):
        count = 1
        for size, _ in routes[r][:stage]:
            count = count * size
        return count

    def send_stage(a, r, stage):
        size, stride = routes[r][stage]
        done = routes[r][:stage]

        def step(i, carry):
            t, d = lax.div(i, size - 1), lax.rem(i, size - 1) + 1
            block = me
            for done_size, done_stride in done:
                block = moved(block, done_size, done_stride, done_size - lax.rem(t, done_size))
                t = lax.div(t, done_size)
            pltpu.make_async_remote_copy(
                src_ref=xg.at[a, r, block],
                dst_ref=xg.at[a, r, block],
                send_sem=ag_send.at[a, r],
                recv_sem=ag_recv.at[a, r, stage],
                device_id={"dp": moved(me, size, stride, d)},
                device_id_type=MESH,
            ).start()
            return carry

        lax.fori_loop(0, held_before(r, stage) * (size - 1), step, 0)

    def take_stage(a, r, stage):
        count = held_before(r, stage) * (routes[r][stage][0] - 1)
        blocks = xg.at[a, r, pl.ds(0, count)]
        pltpu.make_async_copy(blocks, blocks, ag_recv.at[a, r, stage]).wait()

    stages = len(routes[0])
    for a in range(2):
        for r in range(ROUTES):
            send_stage(a, r, 0)
    for stage in range(1, stages):
        for r in range(ROUTES):
            take_stage(0, r, stage - 1)
            send_stage(0, r, stage)

    def lay_out(a, r, q):
        c = r * per_route + q
        group = 16 // own_rows

        def step(g, carry):
            pieces = [
                xg[a, r, g * group + i, :, pl.ds(pl.multiple_of(q * width, width), width)].astype(jnp.float32)
                for i in range(group)
            ]
            xs[a, c, pl.ds(pl.multiple_of(g * 16, 16), 16), :] = jnp.concatenate(pieces, 0).astype(
                jnp.bfloat16
            )
            return carry

        lax.fori_loop(0, tokens // 16, step, 0)

    contract = (((1,), (1,)), ((), ()))

    def add_product(acc, a, m, c):
        acc[...] += lax.dot_general(
            xs[a, c], wbuf[m, c], contract, preferred_element_type=jnp.float32
        )

    gacc[...] = jnp.zeros_like(gacc)
    uacc[...] = jnp.zeros_like(uacc)
    dacc[...] = jnp.zeros_like(dacc)
    def relay(stage):
        if stage < stages:
            for r in range(ROUTES):
                take_stage(1, r, stage - 1)
                send_stage(1, r, stage)

    for r in range(ROUTES):
        take_stage(0, r, stages - 1)

        def gate_up(q, carry, r=r):
            c = r * per_route + q
            lay_out(0, r, q)
            weight_copy(0, c).wait()
            add_product(gacc, 0, 0, c)
            weight_copy(1, c).wait()
            add_product(uacc, 0, 1, c)
            return carry

        for part_of in range(2):
            relay(2 * r + part_of + 1)
            first = part_of * per_route // 2
            lax.fori_loop(first, first + per_route // 2, gate_up, 0)

    for r in range(ROUTES):
        take_stage(1, r, stages - 1)

        def down(q, carry, r=r):
            c = r * per_route + q
            lay_out(1, r, q)
            weight_copy(2, c).wait()
            add_product(dacc, 1, 2, c)
            return carry

        lax.fori_loop(0, per_route, down, 0)

    in_down = out_gate = out_up = jnp.zeros((tokens, rank), jnp.float32)
    for off in range(0, hidden_units, 256):
        cols = slice(off, min(off + 256, hidden_units))
        gate, up, grad = gacc[:, cols], uacc[:, cols], dacc[:, cols]
        sig = jax.nn.sigmoid(gate)
        silu = gate * sig
        hidden = (silu * up).astype(jnp.bfloat16)
        grad_gate = (grad * up * sig * (1.0 + gate * (1.0 - sig))).astype(jnp.bfloat16)
        grad_up = (grad * silu).astype(jnp.bfloat16)
        ph = ph_ref[cols, :]
        in_down += jnp.dot(hidden, ph[:, :rank], preferred_element_type=jnp.float32)
        out_gate += jnp.dot(grad_gate, ph[:, rank : 2 * rank], preferred_element_type=jnp.float32)
        out_up += jnp.dot(grad_up, ph[:, 2 * rank :], preferred_element_type=jnp.float32)

    window = pm_ref.shape[0]
    model_cols = CHUNKS * width // n
    start = lax.div(me * model_cols, window) * window
    own_chunk = lax.div(start, width)
    own_cols = pl.ds(pl.multiple_of(lax.rem(start, width), window), window)
    pm = pm_ref[...]
    rights = jnp.dot(xs[0, own_chunk, :, own_cols], pm[:, : 2 * rank], preferred_element_type=jnp.float32)
    out_down = jnp.dot(xs[1, own_chunk, :, own_cols], pm[:, 2 * rank :], preferred_element_type=jnp.float32)
    part[:, : 2 * rank] = jnp.concatenate([out_gate, out_up], 1)
    part[:, 2 * rank : 4 * rank] = jnp.concatenate([in_down, out_down], 1)
    part[:, 4 * rank :] = rights

    odd = lax.rem(me, 2)
    mine = lax.div(me, 2)

    def rows(j):
        return pl.ds(pl.multiple_of(j * 8, 8), 8)

    def to_reducer(d):
        j = lax.rem(mine + d, half)
        return pltpu.make_async_remote_copy(
            src_ref=part.at[rows(j)],
            dst_ref=rsbuf.at[me],
            send_sem=rs_send,
            recv_sem=rs_recv,
            device_id={"dp": 2 * j},
            device_id_type=MESH,
        )

    def scatter(d, carry):
        to_reducer(d).start()
        return carry

    lax.fori_loop(1, half, scatter, 0)

    @pl.when(odd == 1)
    def _():
        to_reducer(0).start()
        pltpu.make_async_copy(part, part, rs_send).wait()

    @pl.when(odd == 0)
    def _():
        pltpu.make_async_copy(part.at[rows(mine)], rsbuf.at[me], rs_recv).start()
        sent = part.at[pl.ds(0, 8 * (half - 1))]
        pltpu.make_async_copy(sent, sent, rs_send).wait()
        pltpu.make_async_copy(rsbuf, rsbuf, rs_recv).wait()
        red[...] = jnp.sum(rsbuf[...], 0)
        pltpu.make_async_copy(red, vg.at[rows(mine)], bc_recv).start()

        def share(d, carry):
            pltpu.make_async_remote_copy(
                src_ref=red,
                dst_ref=vg.at[rows(mine)],
                send_sem=bc_send,
                recv_sem=bc_recv,
                device_id={"dp": lax.rem(me + d, n)},
                device_id_type=MESH,
            ).start()
            return carry

        lax.fori_loop(1, n, share, 0)
        sent = rsbuf.at[pl.ds(0, n - 1)]
        pltpu.make_async_copy(sent, sent, bc_send).wait()

    for a in range(2):
        for r in range(ROUTES):
            count = 0
            for stage in range(stages):
                count += held_before(r, stage) * (routes[r][stage][0] - 1)
            sent = xg.at[a, r, pl.ds(0, count)]
            pltpu.make_async_copy(sent, sent, ag_send.at[a, r]).wait()

    pltpu.make_async_copy(vg, vg, bc_recv).wait()

    seq = seq_ref[...]
    outs = vg[:, : 2 * rank].T
    mixed = vg[:, 2 * rank : 4 * rank]
    ins = vg[:, 4 * rank :]
    lefts = (outs[:rank], outs[rank:], mixed.T[:rank])
    rights = (ins[:, :rank], ins[:, rank:], mixed[:, rank:])
    for k in range(3):
        left, right = lefts[k], rights[k]
        left_hi = left.astype(jnp.bfloat16).astype(jnp.float32)
        left_lo = left - left_hi
        for s in range(SEQS):
            here = seq == s
            hi = jnp.where(here, left_hi, 0.0).astype(jnp.bfloat16)
            lo = jnp.where(here, left_lo, 0.0).astype(jnp.bfloat16)
            block = slice(s * rank, (s + 1) * rank)
            lm[block, :tokens] = hi
            lm[block, tokens : 2 * tokens] = lo
            lm[block, 2 * tokens :] = hi
        right_hi = right.astype(jnp.bfloat16)
        right_lo = (right - right_hi.astype(jnp.float32)).astype(jnp.bfloat16)
        sketch = jnp.dot(
            lm[...], jnp.concatenate([right_hi, right_hi, right_lo], 0), preferred_element_type=jnp.float32
        )
        sk_ref[:, k] = sketch.reshape(SEQS, rank, rank)

    examples = tgt_ref.shape[0]

    def score(s, carry):
        squares = jnp.zeros((1, rank), jnp.float32)
        sums = [squares] * examples
        for k in range(3):
            block = sk_ref[s, k]
            squares = squares + jnp.sum(block * block, 0, keepdims=True)
            for e in range(examples):
                sums[e] = sums[e] + jnp.sum(block * tgt_ref[e, k].astype(jnp.float32), 0, keepdims=True)
        for e in range(examples):
            prod[e, pl.ds(s, 1), :] = sums[e]
        prod[examples, pl.ds(s, 1), :] = squares
        return carry

    lax.fori_loop(0, SEQS, score, 0)
    lane = lax.broadcasted_iota(jnp.int32, (SEQS, 128), 1)
    folded = jnp.zeros((SEQS, 128), jnp.float32)
    for e in range(examples):
        column = jnp.sum(prod[e], 1, keepdims=True)
        domain = dom_ref[e]
        folded += jnp.where(lane == domain, column, 0.0)
        folded += jnp.where(lane == domain + DOMAINS, 1.0, 0.0)
    inverse_norm = lax.rsqrt(jnp.sum(prod[examples], 1, keepdims=True) + 1e-06)
    msg[...] = folded
    pltpu.make_async_copy(msg, msgbuf.at[me], sc_recv).start()

    def spread(d, carry):
        pltpu.make_async_remote_copy(
            src_ref=msg,
            dst_ref=msgbuf.at[me],
            send_sem=sc_send,
            recv_sem=sc_recv,
            device_id={"dp": lax.rem(me + d, n)},
            device_id_type=MESH,
        ).start()
        return carry

    lax.fori_loop(1, n, spread, 0)
    sent = msgbuf.at[pl.ds(0, n - 1)]
    pltpu.make_async_copy(sent, sent, sc_send).wait()
    pltpu.make_async_copy(msgbuf, msgbuf, sc_recv).wait()
    total = jnp.sum(msgbuf[...], 0)
    score_ref[...] = total[:, :DOMAINS] / total[:, DOMAINS : 2 * DOMAINS] * inverse_norm


def on_device(n, activations, cotangent, w_gate, w_up, w_down, proj_model, proj_hidden, seq_ids, targets, target_domain):
    own_rows, model = activations.shape
    tokens = n * own_rows
    hidden_units = w_gate.shape[0]
    model_cols, features = proj_model.shape
    rank = features // 3
    width = model // CHUNKS
    stages = len(routes_of(n)[0])

    def by_route(x):
        return x.reshape(own_rows, ROUTES, model // ROUTES).transpose(1, 0, 2)

    if model_cols < 128:
        me = lax.axis_index("dp")
        padded = jnp.zeros((128, features), proj_model.dtype)
        proj_model = lax.dynamic_update_slice(padded, proj_model, ((me * model_cols) % 128, 0))
    vmem = pl.BlockSpec(memory_space=pltpu.VMEM)
    hbm = pl.BlockSpec(memory_space=pl.ANY)
    smem = pl.BlockSpec(memory_space=pltpu.SMEM)
    f32, bf16 = jnp.float32, jnp.bfloat16
    dma = pltpu.SemaphoreType.DMA
    return pl.pallas_call(
        functools.partial(kernel, n),
        out_shape=(
            jax.ShapeDtypeStruct((SEQS, 3, rank, rank), f32),
            jax.ShapeDtypeStruct((SEQS, DOMAINS), f32),
        ),
        in_specs=[vmem, vmem, hbm, hbm, hbm, vmem, vmem, vmem, vmem, smem],
        out_specs=(vmem, vmem),
        scratch_shapes=[
            pltpu.VMEM((3, CHUNKS, hidden_units, width), bf16),
            pltpu.VMEM((2, ROUTES, n, own_rows, model // ROUTES), bf16),
            pltpu.VMEM((2, CHUNKS, tokens, width), bf16),
            pltpu.VMEM((tokens, hidden_units), f32),
            pltpu.VMEM((tokens, hidden_units), f32),
            pltpu.VMEM((tokens, hidden_units), f32),
            pltpu.VMEM((tokens, 2 * features), f32),
            pltpu.VMEM((n, 8, 2 * features), f32),
            pltpu.VMEM((8, 2 * features), f32),
            pltpu.VMEM((tokens, 2 * features), f32),
            pltpu.VMEM((SEQS * rank, 3 * tokens), bf16),
            pltpu.VMEM((targets.shape[0] + 1, SEQS, rank), f32),
            pltpu.VMEM((SEQS, 128), f32),
            pltpu.VMEM((n, SEQS, 128), f32),
            dma((3, CHUNKS)),
            dma((2, ROUTES)),
            dma((2, ROUTES)),
            dma((2, ROUTES, stages)),
            dma(()),
            dma(()),
            dma(()),
            dma(()),
            dma(()),
            dma(()),
        ],
        compiler_params=pltpu.CompilerParams(
            collective_id=0, has_side_effects=True, vmem_limit_bytes=67000000
        ),
        name="sketch_scores",
    )(
        by_route(activations), by_route(cotangent), w_gate, w_up, w_down, proj_model, proj_hidden,
        seq_ids.reshape(1, tokens), targets, target_domain,
    )


def solution(mesh):
    in_specs = (
        P(("groups", "dp"), None),
        P(("groups", "dp"), None),
        P("dp", None),
        P("dp", None),
        P("dp", None),
        P("dp", None),
        P("dp", None),
        P("groups"),
        P(("groups", "dp"), None, None, None),
        P(("groups", "dp")),
    )
    out_specs = (P("groups", None, None, None), P("groups", None))
    return jax.shard_map(
        functools.partial(on_device, mesh.shape["dp"]),
        mesh=mesh, in_specs=in_specs, out_specs=out_specs, check_vma=False,
    )
```

```python
import functools

import jax
import jax.numpy as jnp
from jax import lax
from jax.experimental import pallas as pl
from jax.experimental.pallas import tpu as pltpu
from jax.sharding import PartitionSpec as P

DOMAINS = 32
SEQS = 16
MESH = pl.DeviceIdType.MESH
ROUTES = 2
CHUNKS = 8


def routes_of(n):
    core = (2, 1)
    if n == 32:
        z, y, x = (4, 8), (2, 4), (2, 2)
        return ((z, y, x, core), (z, x, y, core))
    if n == 128:
        y, x = (8, 16), (8, 2)
        return ((y, x, core), (x, y, core))
    rest = (n // 2, 2)
    return ((rest, core), (rest, core))


def moved(index, size, stride, by):
    coord = lax.rem(lax.div(index, stride), size)
    return index + (lax.rem(coord + by, size) - coord) * stride


def kernel(
    n,
    act_ref, cot_ref, wg_ref, wu_ref, wd_ref, pm_ref, ph_ref, seq_ref, tgt_ref, dom_ref,
    sk_ref, score_ref,
    wbuf, xg, xs, gacc, uacc, dacc, part, rsbuf, red, vg, lm, tf, prod, msg, msgbuf,
    w_sem, own_sem, ag_send, ag_recv, rs_send, rs_recv, bc_send, bc_recv, sc_send, sc_recv,
):
    me = lax.axis_index("dp")
    half = n // 2
    routes = routes_of(n)
    tokens, width = xs.shape[2], xs.shape[3]
    per_route = CHUNKS // ROUTES
    rank = pm_ref.shape[1] // 3
    hidden_units = wg_ref.shape[0]
    own_rows = act_ref.shape[1]

    def weight_copy(m, c):
        source = (wg_ref, wu_ref, wd_ref)[m]
        return pltpu.make_async_copy(
            source.at[:, pl.ds(c * width, width)], wbuf.at[m, c], w_sem.at[m, c]
        )

    own_copies = []
    for a, source in enumerate((act_ref, cot_ref)):
        for r in range(ROUTES):
            copy = pltpu.make_async_copy(source.at[r], xg.at[a, r, me], own_sem.at[a, r])
            copy.start()
            own_copies.append(copy)

    barrier = pltpu.get_barrier_semaphore()

    def greet(d, carry):
        pl.semaphore_signal(
            barrier, inc=1, device_id={"dp": lax.rem(me + d, n)}, device_id_type=MESH
        )
        return carry

    lax.fori_loop(1, n, greet, 0)
    for c in range(CHUNKS):
        weight_copy(0, c).start()
        weight_copy(1, c).start()
    for c in range(CHUNKS):
        weight_copy(2, c).start()
    for copy in own_copies:
        copy.wait()
    pl.semaphore_wait(barrier, n - 1)

    def held_before(r, stage):
        count = 1
        for size, _ in routes[r][:stage]:
            count = count * size
        return count

    def send_stage(a, r, stage):
        size, stride = routes[r][stage]
        done = routes[r][:stage]

        def step(i, carry):
            t, d = lax.div(i, size - 1), lax.rem(i, size - 1) + 1
            block = me
            for done_size, done_stride in done:
                block = moved(block, done_size, done_stride, done_size - lax.rem(t, done_size))
                t = lax.div(t, done_size)
            pltpu.make_async_remote_copy(
                src_ref=xg.at[a, r, block],
                dst_ref=xg.at[a, r, block],
                send_sem=ag_send.at[a, r],
                recv_sem=ag_recv.at[a, r, stage],
                device_id={"dp": moved(me, size, stride, d)},
                device_id_type=MESH,
            ).start()
            return carry

        lax.fori_loop(0, held_before(r, stage) * (size - 1), step, 0)

    def take_stage(a, r, stage):
        count = held_before(r, stage) * (routes[r][stage][0] - 1)
        blocks = xg.at[a, r, pl.ds(0, count)]
        pltpu.make_async_copy(blocks, blocks, ag_recv.at[a, r, stage]).wait()

    stages = len(routes[0])
    for a in range(2):
        for r in range(ROUTES):
            send_stage(a, r, 0)
    examples = tgt_ref.shape[0]
    for e in range(examples):
        tf[e] = tgt_ref[e].astype(jnp.float32)
    for stage in range(1, stages):
        for r in range(ROUTES):
            take_stage(0, r, stage - 1)
            send_stage(0, r, stage)

    def lay_out(a, r, q):
        c = r * per_route + q
        group = 16 // own_rows

        def step(g, carry):
            pieces = [
                xg[a, r, g * group + i, :, pl.ds(pl.multiple_of(q * width, width), width)].astype(jnp.float32)
                for i in range(group)
            ]
            xs[a, c, pl.ds(pl.multiple_of(g * 16, 16), 16), :] = jnp.concatenate(pieces, 0).astype(
                jnp.bfloat16
            )
            return carry

        lax.fori_loop(0, tokens // 16, step, 0, unroll=True)

    contract = (((1,), (1,)), ((), ()))

    def add_product(acc, a, m, c):
        acc[...] += lax.dot_general(
            xs[a, c], wbuf[m, c], contract, preferred_element_type=jnp.float32
        )

    gacc[...] = jnp.zeros_like(gacc)
    uacc[...] = jnp.zeros_like(uacc)
    dacc[...] = jnp.zeros_like(dacc)
    def relay(stage):
        if stage < stages:
            for r in range(ROUTES):
                take_stage(1, r, stage - 1)
                send_stage(1, r, stage)

    for r in range(ROUTES):
        take_stage(0, r, stages - 1)

        def gate_up(q, carry, r=r):
            c = r * per_route + q
            lay_out(0, r, q)
            weight_copy(0, c).wait()
            add_product(gacc, 0, 0, c)
            weight_copy(1, c).wait()
            add_product(uacc, 0, 1, c)
            return carry

        for part_of in range(2):
            relay(2 * r + part_of + 1)
            first = part_of * per_route // 2
            lax.fori_loop(first, first + per_route // 2, gate_up, 0)

    for r in range(ROUTES):
        take_stage(1, r, stages - 1)

        def down(q, carry, r=r):
            c = r * per_route + q
            lay_out(1, r, q)
            weight_copy(2, c).wait()
            add_product(dacc, 1, 2, c)
            return carry

        lax.fori_loop(0, per_route, down, 0)

    in_down = out_gate = out_up = jnp.zeros((tokens, rank), jnp.float32)
    for off in range(0, hidden_units, 256):
        cols = slice(off, min(off + 256, hidden_units))
        gate, up, grad = gacc[:, cols], uacc[:, cols], dacc[:, cols]
        sig = jax.nn.sigmoid(gate)
        silu = gate * sig
        hidden = (silu * up).astype(jnp.bfloat16)
        grad_gate = (grad * up * sig * (1.0 + gate * (1.0 - sig))).astype(jnp.bfloat16)
        grad_up = (grad * silu).astype(jnp.bfloat16)
        ph = ph_ref[cols, :]
        in_down += jnp.dot(hidden, ph[:, :rank], preferred_element_type=jnp.float32)
        out_gate += jnp.dot(grad_gate, ph[:, rank : 2 * rank], preferred_element_type=jnp.float32)
        out_up += jnp.dot(grad_up, ph[:, 2 * rank :], preferred_element_type=jnp.float32)

    window = pm_ref.shape[0]
    model_cols = CHUNKS * width // n
    start = lax.div(me * model_cols, window) * window
    own_chunk = lax.div(start, width)
    own_cols = pl.ds(pl.multiple_of(lax.rem(start, width), window), window)
    pm = pm_ref[...]
    rights = jnp.dot(xs[0, own_chunk, :, own_cols], pm[:, : 2 * rank], preferred_element_type=jnp.float32)
    out_down = jnp.dot(xs[1, own_chunk, :, own_cols], pm[:, 2 * rank :], preferred_element_type=jnp.float32)
    part[:, : 2 * rank] = jnp.concatenate([out_gate, out_up], 1)
    part[:, 2 * rank : 4 * rank] = jnp.concatenate([in_down, out_down], 1)
    part[:, 4 * rank :] = rights

    odd = lax.rem(me, 2)
    mine = lax.div(me, 2)

    def rows(j):
        return pl.ds(pl.multiple_of(j * 8, 8), 8)

    def to_reducer(d):
        j = lax.rem(mine + d, half)
        return pltpu.make_async_remote_copy(
            src_ref=part.at[rows(j)],
            dst_ref=rsbuf.at[me],
            send_sem=rs_send,
            recv_sem=rs_recv,
            device_id={"dp": 2 * j},
            device_id_type=MESH,
        )

    def scatter(d, carry):
        to_reducer(d).start()
        return carry

    lax.fori_loop(1, half, scatter, 0)

    @pl.when(odd == 1)
    def _():
        to_reducer(0).start()
        pltpu.make_async_copy(part, part, rs_send).wait()

    @pl.when(odd == 0)
    def _():
        pltpu.make_async_copy(part.at[rows(mine)], rsbuf.at[me], rs_recv).start()
        sent = part.at[pl.ds(0, 8 * (half - 1))]
        pltpu.make_async_copy(sent, sent, rs_send).wait()
        pltpu.make_async_copy(rsbuf, rsbuf, rs_recv).wait()
        red[...] = jnp.sum(rsbuf[...], 0)
        pltpu.make_async_copy(red, vg.at[rows(mine)], bc_recv).start()

        def share(d, carry):
            pltpu.make_async_remote_copy(
                src_ref=red,
                dst_ref=vg.at[rows(mine)],
                send_sem=bc_send,
                recv_sem=bc_recv,
                device_id={"dp": lax.rem(me + d, n)},
                device_id_type=MESH,
            ).start()
            return carry

        lax.fori_loop(1, n, share, 0)
        sent = rsbuf.at[pl.ds(0, n - 1)]
        pltpu.make_async_copy(sent, sent, bc_send).wait()

    for a in range(2):
        for r in range(ROUTES):
            count = 0
            for stage in range(stages):
                count += held_before(r, stage) * (routes[r][stage][0] - 1)
            sent = xg.at[a, r, pl.ds(0, count)]
            pltpu.make_async_copy(sent, sent, ag_send.at[a, r]).wait()

    pltpu.make_async_copy(vg, vg, bc_recv).wait()

    seq = seq_ref[...]
    outs = vg[:, : 2 * rank].T
    mixed = vg[:, 2 * rank : 4 * rank]
    ins = vg[:, 4 * rank :]
    lefts = (outs[:rank], outs[rank:], mixed.T[:rank])
    rights = (ins[:, :rank], ins[:, rank:], mixed[:, rank:])
    for k in range(3):
        left, right = lefts[k], rights[k]
        left_hi = left.astype(jnp.bfloat16).astype(jnp.float32)
        left_lo = left - left_hi
        for s in range(SEQS):
            here = seq == s
            hi = jnp.where(here, left_hi, 0.0).astype(jnp.bfloat16)
            lo = jnp.where(here, left_lo, 0.0).astype(jnp.bfloat16)
            block = slice(s * rank, (s + 1) * rank)
            lm[block, :tokens] = hi
            lm[block, tokens : 2 * tokens] = lo
            lm[block, 2 * tokens :] = hi
        right_hi = right.astype(jnp.bfloat16)
        right_lo = (right - right_hi.astype(jnp.float32)).astype(jnp.bfloat16)
        sketch = jnp.dot(
            lm[...], jnp.concatenate([right_hi, right_hi, right_lo], 0), preferred_element_type=jnp.float32
        )
        sk_ref[:, k] = sketch.reshape(SEQS, rank, rank)

    def score(s, carry):
        squares = jnp.zeros((8, rank), jnp.float32)
        sums = [squares] * examples
        for k in range(3):
            block = sk_ref[s, k]
            for i in range(0, rank, 8):
                piece = block[i : i + 8]
                squares = squares + piece * piece
                for e in range(examples):
                    sums[e] = sums[e] + piece * tf[e, k, i : i + 8, :]
        for e in range(examples):
            prod[e, s] = sums[e]
        prod[examples, s] = squares
        return carry

    lax.fori_loop(0, SEQS, score, 0)

    def column_of(e):
        return jnp.sum(jnp.sum(prod[e], 1), 1, keepdims=True)

    top = SEQS // 2
    lane = lax.broadcasted_iota(jnp.int32, (top, 128), 1)
    folded = jnp.zeros((top, 128), jnp.float32)
    for e in range(examples):
        column = column_of(e)
        domain = dom_ref[e]
        folded += jnp.where(lane == domain, column[:top], 0.0)
        folded += jnp.where(lane == domain + DOMAINS, column[top:], 0.0)
        folded += jnp.where(lane == domain + 2 * DOMAINS, 1.0, 0.0)
    inverse_norm = lax.rsqrt(column_of(examples) + 1e-06)
    msg[...] = folded
    pltpu.make_async_copy(msg, msgbuf.at[me], sc_recv).start()

    def spread(d, carry):
        pltpu.make_async_remote_copy(
            src_ref=msg,
            dst_ref=msgbuf.at[me],
            send_sem=sc_send,
            recv_sem=sc_recv,
            device_id={"dp": lax.rem(me + d, n)},
            device_id_type=MESH,
        ).start()
        return carry

    lax.fori_loop(1, n, spread, 0)
    sent = msgbuf.at[pl.ds(0, n - 1)]
    pltpu.make_async_copy(sent, sent, sc_send).wait()
    pltpu.make_async_copy(msgbuf, msgbuf, sc_recv).wait()
    total = jnp.sum(msgbuf[...], 0)
    counts = total[:, 2 * DOMAINS : 3 * DOMAINS]
    score_ref[:top] = total[:, :DOMAINS] / counts * inverse_norm[:top]
    score_ref[top:] = total[:, DOMAINS : 2 * DOMAINS] / counts * inverse_norm[top:]


def on_device(n, activations, cotangent, w_gate, w_up, w_down, proj_model, proj_hidden, seq_ids, targets, target_domain):
    own_rows, model = activations.shape
    tokens = n * own_rows
    hidden_units = w_gate.shape[0]
    model_cols, features = proj_model.shape
    rank = features // 3
    width = model // CHUNKS
    stages = len(routes_of(n)[0])

    def by_route(x):
        return x.reshape(own_rows, ROUTES, model // ROUTES).transpose(1, 0, 2)

    if model_cols < 128:
        me = lax.axis_index("dp")
        padded = jnp.zeros((128, features), proj_model.dtype)
        proj_model = lax.dynamic_update_slice(padded, proj_model, ((me * model_cols) % 128, 0))
    vmem = pl.BlockSpec(memory_space=pltpu.VMEM)
    hbm = pl.BlockSpec(memory_space=pl.ANY)
    smem = pl.BlockSpec(memory_space=pltpu.SMEM)
    f32, bf16 = jnp.float32, jnp.bfloat16
    dma = pltpu.SemaphoreType.DMA
    return pl.pallas_call(
        functools.partial(kernel, n),
        out_shape=(
            jax.ShapeDtypeStruct((SEQS, 3, rank, rank), f32),
            jax.ShapeDtypeStruct((SEQS, DOMAINS), f32),
        ),
        in_specs=[vmem, vmem, hbm, hbm, hbm, vmem, vmem, vmem, vmem, smem],
        out_specs=(vmem, vmem),
        scratch_shapes=[
            pltpu.VMEM((3, CHUNKS, hidden_units, width), bf16),
            pltpu.VMEM((2, ROUTES, n, own_rows, model // ROUTES), bf16),
            pltpu.VMEM((2, CHUNKS, tokens, width), bf16),
            pltpu.VMEM((tokens, hidden_units), f32),
            pltpu.VMEM((tokens, hidden_units), f32),
            pltpu.VMEM((tokens, hidden_units), f32),
            pltpu.VMEM((tokens, 2 * features), f32),
            pltpu.VMEM((n, 8, 2 * features), f32),
            pltpu.VMEM((8, 2 * features), f32),
            pltpu.VMEM((tokens, 2 * features), f32),
            pltpu.VMEM((SEQS * rank, 3 * tokens), bf16),
            pltpu.VMEM(targets.shape, f32),
            pltpu.VMEM((targets.shape[0] + 1, SEQS, 8, rank), f32),
            pltpu.VMEM((SEQS // 2, 128), f32),
            pltpu.VMEM((n, SEQS // 2, 128), f32),
            dma((3, CHUNKS)),
            dma((2, ROUTES)),
            dma((2, ROUTES)),
            dma((2, ROUTES, stages)),
            dma(()),
            dma(()),
            dma(()),
            dma(()),
            dma(()),
            dma(()),
        ],
        compiler_params=pltpu.CompilerParams(
            collective_id=0, has_side_effects=True, vmem_limit_bytes=67000000
        ),
        name="sketch_scores",
    )(
        by_route(activations), by_route(cotangent), w_gate, w_up, w_down, proj_model, proj_hidden,
        seq_ids.reshape(1, tokens), targets, target_domain,
    )


def solution(mesh):
    in_specs = (
        P(("groups", "dp"), None),
        P(("groups", "dp"), None),
        P("dp", None),
        P("dp", None),
        P("dp", None),
        P("dp", None),
        P("dp", None),
        P("groups"),
        P(("groups", "dp"), None, None, None),
        P(("groups", "dp")),
    )
    out_specs = (P("groups", None, None, None), P("groups", None))
    return jax.shard_map(
        functools.partial(on_device, mesh.shape["dp"]),
        mesh=mesh, in_specs=in_specs, out_specs=out_specs, check_vma=False,
    )
```
